32 devices in a mesh: req: 16 (over z, y, x), tp: 2 (over core).
Axes of the slice: x: 2, y: 2, z: 4, core: 2. Of those that a mesh axis runs over, the one named last changes fastest.
Arguments:
- tokens: bfloat16 [8192, 1664], P('req'), may hold values from -6 to 6
- qkv_weight: bfloat16 [1664, 3, 1664], P('req', None, 'tp')
- out_weight: bfloat16 [1664, 1664], P('tp', 'req'), may hold values from -0.15625 to 0.15625
- fc1_weight: bfloat16 [1664, 8192], P('req', 'tp'), may hold values from -0.15625 to 0.15625
- fc2_weight: bfloat16 [8192, 1664], P('tp', 'req'), may hold values from -0.0625 to 0.0625
- norm1_gain: float32 [1664], replicated, may hold values from 0.1 to 1.9
- norm2_gain: float32 [1664], replicated, may hold values from 0.1 to 1.9
- norm3_gain: float32 [1664], replicated, may hold values from 0.1 to 1.9
- proj_weight: bfloat16 [6656, 4096], P('req', 'tp'), may hold values from -0.078125 to 0.078125
- grid_h: int32 [32], replicated, may hold values from 2 to 16, as said below
- grid_w: int32 [32], replicated, may hold values from 2 to 16, as said below
- segment_ids: int32 [8192], P('req'), may hold values from 0 to 2, as said below
- patch_mask: int32 [8192], P('req'), may hold values from 0 to 1, as said below
- owner: int32 [32], replicated, may hold values from 0 to 15, as said below
Outputs:
- embedded: bfloat16 [2048, 4096], P('req', 'tp')
- pooled_norm: float32 [32], P('req')
- top_logit: float32 [32], P('req')
The draws below stay inside these ranges and needn't reach their ends.
Inputs may be any that keep to these rules, and one draw needn't show every extreme that they name: `grid_h`: Even. On one req index every request has height 16 and width 16, so that its requests fill all 512 rows. `grid_w`: Even. `segment_ids`: within the 512 rows of each req index, the j-th request of that index covers the next grid_h * grid_w rows with id j, from the first row on; the remaining rows carry id 2. `patch_mask`: 0 on every row with segment id 2. `owner`: the 2 requests of req index i are owned by the indices (i + o) mod the req axis's size, each o from 0 to 1 once.
All inputs are finite; a program needn't handle non-finite values.
Results may differ from the reference program's by a relative error of at most 0.0085.
The reference program's roundings to bfloat16 on the way count: a program that leaves them out, or rounds other values in their place, can miss the bound.
Values may be sent and summed in bfloat16 or wider, within the bound.
A program may use at most 128 MiB of HBM per device.

```python
import math
import jax
import jax.numpy as jnp
from jax import lax

D = 1664
HD = 104
FF = 8192
OUT = 4096
GH_MAX = 16
GW_MAX = 16
REQ_DEV = 2
TOK_DEV = 512
MCAP = 64
MERGED = 6656
REQUESTS = 32
TOKENS = 8192


def layout(key):
    devices = REQUESTS // REQ_DEV
    keys = jax.random.split(jax.random.fold_in(key, 7), 5)
    heights = 2 * jax.random.randint(keys[0], (devices, REQ_DEV), 1, GH_MAX // 2 + 1)
    widths = 2 * jax.random.randint(keys[1], (devices, REQ_DEV), 1, GW_MAX // 2 + 1)
    chosen = jax.random.randint(keys[2], (), 0, devices)
    filled = (jnp.arange(devices) == chosen)[:, None]
    heights = jnp.where(filled, GH_MAX, heights).astype(jnp.int32)
    widths = jnp.where(filled, GW_MAX, widths).astype(jnp.int32)
    ends = jnp.cumsum(heights * widths, axis=1)
    places = jnp.arange(TOK_DEV)
    segs = jnp.sum((places[None, None, :] >= ends[:, :, None]).astype(jnp.int32), axis=1)
    keep = (jax.random.randint(keys[3], (devices, TOK_DEV), 0, 8) > 0) & (segs < REQ_DEV)
    ranks = jax.random.randint(keys[4], (devices, REQ_DEV), 0, 1024) * REQ_DEV + jnp.arange(REQ_DEV)[None, :]
    order = jnp.argsort(ranks, axis=1)
    owners = jnp.mod(jnp.arange(devices)[:, None] + order, devices)
    return (heights.reshape(-1), widths.reshape(-1), segs.reshape(-1).astype(jnp.int32), keep.astype(jnp.int32).reshape(-1), owners.reshape(-1).astype(jnp.int32))


def draw_grid_h(key, part):
    return layout(key)[0]


def draw_grid_w(key, part):
    return layout(key)[1]


def draw_segment_ids(key, part):
    return layout(key)[2]


def draw_patch_mask(key, part):
    return layout(key)[3]


def draw_owner(key, part):
    return layout(key)[4]


def draw_qkv_weight(key, part):
    values = jax.random.normal(key, (D, 3, D), jnp.float32) * D ** (-0.5)
    return values.astype(jnp.bfloat16)


def level_of(rng, extent, cuts, low, high):
    level = 1.0
    for dim, parts in cuts:
        steps = jax.random.uniform(jax.random.fold_in(jax.random.fold_in(rng, 6), dim), (parts,), jnp.float32, low / len(cuts), high / len(cuts))
        level = level * jnp.repeat(jnp.exp(steps), extent[dim] // parts).reshape((-1,) + (1,) * (len(extent) - 1 - dim))
    return level


def normal_values(rng, shape, scale, most, shards=(), kind=jnp.bfloat16):
    level = level_of(rng, shape, shards, -0.22, 0.18) if shards else 1.0
    result = jax.random.normal(rng, shape, jnp.float32) * scale * level
    return jnp.minimum(jnp.maximum(result, -most), most).astype(kind)


def setup_inputs(seed: int = 0) -> dict:
    seeds = jax.random.split(jax.random.key(seed), 15)
    tokens = normal_values(seeds[0], (TOKENS, D), 1.0, 6.0, ((0, 16),))
    qkv_weight = draw_qkv_weight(jax.random.fold_in(seeds[14], 71), 0)
    out_weight = normal_values(seeds[2], (D, D), D ** -0.5, 0.15625, ((0, 2), (1, 16)))
    fc1_weight = normal_values(seeds[3], (D, FF), D ** -0.5, 0.15625, ((0, 16), (1, 2)))
    fc2_weight = normal_values(seeds[4], (FF, D), FF ** -0.5, 0.0625, ((0, 2), (1, 16)))
    norm1_gain = jnp.clip(1.0 + 0.18 * jax.random.normal(seeds[5], (D,), jnp.float32), 0.1, 1.9)
    norm2_gain = jnp.clip(1.0 + 0.18 * jax.random.normal(seeds[6], (D,), jnp.float32), 0.1, 1.9)
    norm3_gain = jnp.clip(1.0 + 0.18 * jax.random.normal(seeds[7], (D,), jnp.float32), 0.1, 1.9)
    proj_weight = normal_values(seeds[8], (MERGED, OUT), MERGED ** -0.5, 0.078125, ((0, 16), (1, 2)))
    grid_h = draw_grid_h(jax.random.fold_in(seeds[14], 71), 0)
    grid_w = draw_grid_w(jax.random.fold_in(seeds[14], 71), 0)
    segment_ids = draw_segment_ids(jax.random.fold_in(seeds[14], 71), 0)
    patch_mask = draw_patch_mask(jax.random.fold_in(seeds[14], 71), 0)
    owner = draw_owner(jax.random.fold_in(seeds[14], 71), 0)
    return {"tokens": tokens, "qkv_weight": qkv_weight, "out_weight": out_weight, "fc1_weight": fc1_weight, "fc2_weight": fc2_weight, "norm1_gain": norm1_gain, "norm2_gain": norm2_gain, "norm3_gain": norm3_gain, "proj_weight": proj_weight, "grid_h": grid_h, "grid_w": grid_w, "segment_ids": segment_ids, "patch_mask": patch_mask, "owner": owner}


EPS = 1e-06

def layer_norm(rows, gain):
    mean = lax.optimization_barrier(jnp.mean(rows, axis=-1, keepdims=True))
    centered = rows - mean
    spread = lax.optimization_barrier(jnp.mean(centered * centered, axis=-1, keepdims=True))
    return (centered * lax.rsqrt(spread + EPS) * gain).astype(jnp.bfloat16)

def attend(qkv_rows, segment_ids, patch_mask, head_dim):
    count = qkv_rows.shape[0]
    heads = qkv_rows.shape[2] // head_dim
    split = qkv_rows.reshape(count, 3, heads, head_dim)
    query = split[:, 0].astype(jnp.float32)
    keys = split[:, 1].astype(jnp.float32)
    values = split[:, 2].astype(jnp.float32)
    scores = jnp.einsum('qhd,khd->hqk', query, keys) / math.sqrt(head_dim)
    places = jnp.arange(count)
    visible = (segment_ids[:, None] == segment_ids[None, :]) & (patch_mask[None, :] > 0) | (places[:, None] == places[None, :])
    scores = jnp.where(visible[None], scores, -1e+30)
    peak = lax.optimization_barrier(jnp.max(scores, axis=-1, keepdims=True))
    weights = jnp.exp(scores - peak)
    total = lax.optimization_barrier(jnp.sum(weights, axis=-1, keepdims=True))
    probs = (weights / total).astype(jnp.bfloat16).astype(jnp.float32)
    mixed = jnp.einsum('hqk,khd->qhd', probs, values)
    return mixed.astype(jnp.bfloat16).reshape(count, heads * head_dim)

def reference(tokens, qkv_weight, out_weight, fc1_weight, fc2_weight, norm1_gain, norm2_gain, norm3_gain, proj_weight, grid_h, grid_w, segment_ids, patch_mask, owner):
    req_count = REQUESTS // REQ_DEV
    qkv_flat = qkv_weight.reshape(D, 3 * D)

    def encode(block):
        rows, segs, masks = block
        resid = rows.astype(jnp.float32)
        normed = layer_norm(resid, norm1_gain)
        qkv_rows = jnp.dot(normed, qkv_flat, preferred_element_type=jnp.float32).astype(jnp.bfloat16).reshape(TOK_DEV, 3, D)
        mixed = attend(qkv_rows, segs, masks, HD)
        resid1 = resid + jnp.dot(mixed, out_weight, preferred_element_type=jnp.float32)
        normed2 = layer_norm(resid1, norm2_gain)
        hidden = jax.nn.gelu(jnp.dot(normed2, fc1_weight, preferred_element_type=jnp.float32), approximate=False).astype(jnp.bfloat16)
        resid2 = resid1 + jnp.dot(hidden, fc2_weight, preferred_element_type=jnp.float32)
        final = layer_norm(resid2, norm3_gain)
        merged = final.reshape(TOK_DEV // 4, 4 * D)
        return jnp.dot(merged, proj_weight, preferred_element_type=jnp.float32)
    projected = lax.map(encode, (tokens.reshape(req_count, TOK_DEV, D), segment_ids.reshape(req_count, TOK_DEV), patch_mask.reshape(req_count, TOK_DEV)))
    merged_len = (grid_h * grid_w // 4).astype(jnp.int32)
    per_dev = merged_len.reshape(req_count, REQ_DEV)
    starts = (jnp.cumsum(per_dev, axis=1) - per_dev).reshape(-1).astype(jnp.int32)
    numbers = jnp.arange(REQUESTS).astype(jnp.int32)
    source_of = numbers // REQ_DEV
    offset_of = jnp.mod(owner - source_of, req_count)
    slot_of = owner * REQ_DEV + offset_of
    match = slot_of[None, :] == numbers[:, None]
    request_of_slot = lax.optimization_barrier(jnp.sum(jnp.where(match, numbers[None, :], 0), axis=1)).astype(jnp.int32)
    source = request_of_slot // REQ_DEV
    start = starts[request_of_slot]
    count = merged_len[request_of_slot]
    steps_idx = jnp.arange(MCAP).astype(jnp.int32)
    index = jnp.minimum(start[:, None] + steps_idx[None, :], TOK_DEV // 4 - 1).astype(jnp.int32)
    rows_out = projected[source[:, None], index]
    rows_out = jnp.where((steps_idx[None, :] < count[:, None])[:, :, None], rows_out, jnp.zeros_like(rows_out))
    pooled = lax.optimization_barrier(jnp.sum(rows_out, axis=1)) / count[:, None].astype(jnp.float32)
    scale = jnp.sqrt(lax.optimization_barrier(jnp.sum(pooled * pooled, axis=1)) / OUT + EPS)
    top = lax.optimization_barrier(jnp.max(pooled, axis=1)) / scale
    return (rows_out.reshape(REQUESTS * MCAP, OUT).astype(jnp.bfloat16), scale, top)
```

```python
import math

import jax
import jax.numpy as jnp
from jax import lax
from jax.sharding import PartitionSpec as P

HD = 104
OUT = 4096


EPS = 1e-06


def shifted(value, axis, steps):
    count = lax.axis_size(axis)
    pairs = [(source, (source + steps) % count) for source in range(count)]
    return lax.ppermute(value, axis, pairs)


def layer_norm(rows, gain):
    mean = jnp.mean(rows, axis=-1, keepdims=True)
    centered = rows - mean
    spread = jnp.mean(centered * centered, axis=-1, keepdims=True)
    return (centered * lax.rsqrt(spread + EPS) * gain).astype(jnp.bfloat16)


def attend(qkv_rows, segment_ids, patch_mask, head_dim):
    count = qkv_rows.shape[0]
    heads = qkv_rows.shape[2] // head_dim
    split = qkv_rows.reshape(count, 3, heads, head_dim)
    query, keys, values = (split[:, 0], split[:, 1], split[:, 2])
    scores = jnp.einsum(
        "qhd,khd->hqk", query, keys, preferred_element_type=jnp.float32
    ) / math.sqrt(head_dim)
    places = jnp.arange(count)
    visible = (segment_ids[:, None] == segment_ids[None, :]) & (patch_mask[None, :] > 0) | (
        places[:, None] == places[None, :]
    )
    scores = jnp.where(visible[None], scores, -1e30)
    peak = jnp.max(scores, axis=-1, keepdims=True)
    weights = jnp.exp(scores - peak)
    total = jnp.sum(weights, axis=-1, keepdims=True)
    probs = (weights / total).astype(jnp.bfloat16)
    mixed = jnp.einsum("hqk,khd->qhd", probs, values, preferred_element_type=jnp.float32)
    return mixed.astype(jnp.bfloat16).reshape(count, heads * head_dim)


def shards(
    tokens,
    qkv_weight,
    out_weight,
    fc1_weight,
    fc2_weight,
    norm1_gain,
    norm2_gain,
    norm3_gain,
    proj_weight,
    grid_h,
    grid_w,
    segment_ids,
    patch_mask,
    owner,
):
    rows = tokens.shape[0]
    width = tokens.shape[1]
    share = rows // lax.axis_size("tp")
    resid = tokens.astype(jnp.float32)
    normed = layer_norm(resid, norm1_gain)
    columns = normed
    qkv_rows = jnp.einsum(
        "rd,dcj->rcj",
        columns,
        lax.all_gather(qkv_weight, "req", axis=0, tiled=True),
        preferred_element_type=jnp.float32,
    ).astype(jnp.bfloat16)
    mixed = attend(qkv_rows, segment_ids, patch_mask, HD)
    attn_part = jnp.dot(
        mixed,
        lax.all_gather(out_weight, "req", axis=1, tiled=True),
        preferred_element_type=jnp.float32,
    )
    first = lax.axis_index("tp") * share
    resid1 = lax.dynamic_slice_in_dim(resid, first, share, 0) + lax.psum_scatter(
        attn_part, "tp", scatter_dimension=0, tiled=True
    )
    normed2 = lax.all_gather(layer_norm(resid1, norm2_gain), "tp", axis=0, tiled=True)
    columns = normed2
    before = jnp.dot(
        columns,
        lax.all_gather(fc1_weight, "req", axis=0, tiled=True),
        preferred_element_type=jnp.float32,
    )
    hidden = jax.nn.gelu(before, approximate=False).astype(jnp.bfloat16)
    resid2 = resid1 + lax.psum_scatter(
        jnp.dot(
            hidden,
            lax.all_gather(fc2_weight, "req", axis=1, tiled=True),
            preferred_element_type=jnp.float32,
        ),
        "tp",
        scatter_dimension=0,
        tiled=True,
    )
    final = lax.all_gather(layer_norm(resid2, norm3_gain), "tp", axis=0, tiled=True)
    merged = final.reshape(rows // 4, 4 * width)
    req_count = lax.axis_size("req")
    here = lax.axis_index("req")
    per_dev = grid_h.shape[0] // req_count
    slots = rows // (4 * per_dev)
    merged_len = grid_h * grid_w // 4
    mine = lax.dynamic_slice_in_dim(merged_len, here * per_dev, per_dev)
    my_owner = lax.dynamic_slice_in_dim(owner, here * per_dev, per_dev)
    my_start = jnp.cumsum(mine) - mine
    offsets = jnp.mod(my_owner - here, req_count)
    pick = offsets[None, :] == jnp.arange(per_dev)[:, None]
    send_start = jnp.sum(jnp.where(pick, my_start[None, :], 0), axis=1)
    send_count = jnp.sum(jnp.where(pick, mine[None, :], 0), axis=1)
    step_index = jnp.arange(slots)
    source_of = jnp.arange(grid_h.shape[0]) // per_dev
    sources = jnp.mod(here - jnp.arange(per_dev), req_count)
    match = (owner[None, :] == here) & (source_of[None, :] == sources[:, None])
    recv_count = jnp.sum(jnp.where(match, merged_len[None, :], 0), axis=1)

    def slot_rows(table, offset):
        index = jnp.minimum(send_start[offset] + step_index, table.shape[0] - 1)
        taken = jnp.take(table, index, axis=0)
        return jnp.where((step_index < send_count[offset])[:, None], taken, jnp.zeros_like(taken))

    def project_rows(inputs):

        def add_proj(total, piece, start):
            return jnp.dot(inputs, piece, preferred_element_type=jnp.float32)

        return (add_proj, jnp.zeros((inputs.shape[0], proj_weight.shape[1]), jnp.float32))

    parcels = [slot_rows(merged, 0)]
    offset = 1
    parcels.append(shifted(slot_rows(merged, offset), "req", offset))
    owned = jnp.concatenate(parcels, axis=0)
    add_proj, proj_init = project_rows(owned)
    projected = add_proj(
        proj_init, lax.all_gather(proj_weight, "req", axis=0, tiled=True), jnp.int32(0)
    )
    blocks = projected.reshape(per_dev, slots, projected.shape[1])
    pooled = jnp.sum(blocks, axis=1) / recv_count[:, None].astype(jnp.float32)
    squares = jnp.sum(pooled * pooled, axis=1)
    largest = jnp.max(pooled, axis=1)
    total_sq = lax.psum(squares, "tp")
    peak = lax.pmax(largest, "tp")
    scale = jnp.sqrt(total_sq / OUT + EPS)
    return (projected.astype(jnp.bfloat16), scale, peak / scale)


def plain_solution(mesh):
    return jax.shard_map(
        shards,
        mesh=mesh,
        in_specs=(
            P("req", None),
            P("req", None, "tp"),
            P("tp", "req"),
            P("req", "tp"),
            P("tp", "req"),
            P(),
            P(),
            P(),
            P("req", "tp"),
            P(),
            P(),
            P("req"),
            P("req"),
            P(),
        ),
        out_specs=(P("req", "tp"), P("req"), P("req")),
        check_vma=False,
    )


def attend_group(qkv_rows, segment_ids, key_ids, head_dim):
    parts, count = segment_ids.shape
    heads = qkv_rows.shape[2] // head_dim
    split = qkv_rows.reshape(parts, count, 3, heads, head_dim)
    query, keys, values = (split[:, :, 0], split[:, :, 1], split[:, :, 2])
    scores = jnp.einsum(
        "gqhd,gkhd->ghqk", query, keys, preferred_element_type=jnp.float32
    ) / math.sqrt(head_dim)
    places = jnp.arange(count)
    visible = (segment_ids[:, :, None] == key_ids[:, None, :]) | (
        places[:, None] == places[None, :]
    )
    scores = jnp.where(visible[:, None], scores, -1e30)
    peak = jnp.max(scores, axis=-1, keepdims=True)
    weights = jnp.exp(scores - peak)
    total = jnp.sum(weights, axis=-1, keepdims=True)
    probs = (weights / total).astype(jnp.bfloat16)
    mixed = jnp.einsum("ghqk,gkhd->gqhd", probs, values, preferred_element_type=jnp.float32)
    return mixed.astype(jnp.bfloat16).reshape(parts * count, heads * head_dim)


def exchange(value, split_axis, concat_axis):
    return lax.all_to_all(value, "near", split_axis, concat_axis, tiled=True)


def ring_pairs(order):
    ahead = [(order[p], order[(p + 1) % 4]) for p in range(4)]
    return ahead, [(target, source) for source, target in ahead]


def ring_first(value, axis, order):
    if lax.axis_size(axis) != 4:
        return (value,)
    ahead, behind = ring_pairs(order)
    return value, lax.ppermute(value, axis, ahead), lax.ppermute(value, axis, behind)


def ring_second(blocks, axis, order):
    if lax.axis_size(axis) != 4:
        return lax.all_gather(blocks[0], axis, axis=0, tiled=False)
    value, left, right = blocks
    ahead, behind = ring_pairs(order)
    half = value.shape[0] // 2
    upper = lax.ppermute(left[:half], axis, ahead)
    lower = lax.ppermute(right[half:], axis, behind)
    me = lax.axis_index(axis)
    names = jnp.array(order)
    place = jnp.sum(jnp.where(names == me, jnp.arange(4), 0))

    def member(steps):
        return jnp.sum(jnp.where(jnp.arange(4) == jnp.mod(place + steps, 4), names, 0))

    out = jnp.zeros((4,) + value.shape, value.dtype)
    rest = (0,) * (value.ndim - 1)
    out = lax.dynamic_update_slice(out, value[None], (me, 0) + rest)
    out = lax.dynamic_update_slice(out, left[None], (member(3), 0) + rest)
    out = lax.dynamic_update_slice(out, right[None], (member(1), 0) + rest)
    out = lax.dynamic_update_slice(out, upper[None], (member(2), 0) + rest)
    return lax.dynamic_update_slice(out, lower[None], (member(2), half) + rest)


LINE = (0, 1, 2, 3)
PLANE = (0, 1, 3, 2)


def far_first(value):
    return ring_first(value, "far", LINE)


def far_second(blocks):
    out = ring_second(blocks, "far", LINE)
    return out.reshape((-1,) + out.shape[2:])


def gather_group(value):
    return lax.all_gather(value, ("near", "tp"), axis=0, tiled=True)


def grouped_shards(
    tokens,
    qkv_weight,
    out_weight,
    fc1_weight,
    fc2_weight,
    norm1_gain,
    norm2_gain,
    norm3_gain,
    proj_weight,
    grid_h,
    grid_w,
    segment_ids,
    patch_mask,
    owner,
):
    rows, width = tokens.shape
    near = lax.axis_size("near")
    req_count = lax.axis_size("far") * near
    group_first = lax.axis_index("far") * near
    here = group_first + lax.axis_index("near")
    share = rows // lax.axis_size("tp")
    first = lax.axis_index("tp") * share

    near_heads = qkv_weight.shape[2] // near
    qkv_cut = qkv_weight.reshape(-1, 3, near, near_heads).transpose(2, 0, 1, 3)
    qkv_cut = qkv_cut.reshape(near * qkv_weight.shape[0], 3 * near_heads)
    qkv_full = far_second(far_first(exchange(qkv_cut, 0, 0)))
    fc1 = exchange(fc1_weight, 1, 0)
    fc2 = exchange(fc2_weight.T, 1, 0)
    proj = exchange(proj_weight, 1, 0)

    ids = jnp.stack([segment_ids, jnp.where(patch_mask > 0, segment_ids, -1)])[None]
    ids = lax.all_gather(ids, "near", axis=0, tiled=True)
    resid = lax.dynamic_slice_in_dim(tokens, first, share, 0).astype(jnp.float32)
    normed = gather_group(layer_norm(resid, norm1_gain))
    normed, fc1, fc2, proj = lax.optimization_barrier((normed, fc1, fc2, proj))
    fc1, fc2 = far_first(fc1), far_first(fc2)
    out_far = ring_second(ring_first(out_weight.T, "far", LINE), "far", LINE)
    out_near = ring_first(out_far, "near", PLANE)
    qkv_rows = jnp.dot(normed, qkv_full, preferred_element_type=jnp.float32).astype(jnp.bfloat16)
    qkv_rows = qkv_rows.reshape(-1, 3, near_heads)
    mixed = attend_group(qkv_rows, ids[:, 0], ids[:, 1], HD)
    mixed, fc1, fc2, out_near = lax.optimization_barrier((mixed, fc1, fc2, out_near))
    mixed = exchange(mixed, 0, 1)
    out_full = jnp.swapaxes(ring_second(out_near, "near", PLANE), 0, 1)
    out_full = out_full.reshape(width, out_weight.shape[0])
    fc1_full, fc2_full = far_second(fc1), far_second(fc2)
    attn_part = jnp.einsum("rk,ck->rc", mixed, out_full, preferred_element_type=jnp.float32)
    resid1 = resid + lax.psum_scatter(attn_part, "tp", scatter_dimension=0, tiled=True)
    resid1, fc1_full, fc2_full, proj = lax.optimization_barrier((resid1, fc1_full, fc2_full, proj))
    proj = far_first(proj)
    normed2 = gather_group(layer_norm(resid1, norm2_gain))
    normed2, proj = lax.optimization_barrier((normed2, proj))
    proj_full = far_second(proj)
    before = jnp.dot(normed2, fc1_full, preferred_element_type=jnp.float32)
    hidden = jax.nn.gelu(before, approximate=False).astype(jnp.bfloat16)
    hidden, proj_full = lax.optimization_barrier((hidden, proj_full))
    resid2 = resid1 + lax.psum_scatter(
        jnp.einsum("rk,ck->rc", hidden, fc2_full, preferred_element_type=jnp.float32),
        ("near", "tp"),
        scatter_dimension=0,
        tiled=True,
    )
    merged = gather_group(layer_norm(resid2, norm3_gain).reshape(share // 4, 4 * width))
    projected = jnp.dot(merged, proj_full, preferred_element_type=jnp.float32)

    per_dev = grid_h.shape[0] // req_count
    places = rows // 4
    slots = places // per_dev
    merged_len = (grid_h * grid_w // 4).reshape(req_count, per_dev)
    starts = jnp.cumsum(merged_len, axis=1) - merged_len
    offsets = jnp.mod(owner.reshape(req_count, per_dev) - jnp.arange(req_count)[:, None], req_count)
    pick = offsets[:, None, :] == jnp.arange(per_dev)[None, :, None]
    slot_start = jnp.sum(jnp.where(pick, starts[:, None, :], 0), axis=2)
    slot_count = jnp.sum(jnp.where(pick, merged_len[:, None, :], 0), axis=2)
    slot_start = lax.dynamic_slice_in_dim(slot_start, group_first, near, 0)
    slot_count = lax.dynamic_slice_in_dim(slot_count, group_first, near, 0)
    step = jnp.arange(slots)
    index = jnp.minimum(slot_start[:, :, None] + step, places - 1)
    index = index + (jnp.arange(near) * places)[:, None, None]
    taken = jnp.take(projected, index.reshape(-1), axis=0)
    live = (step < slot_count[:, :, None]).reshape(-1)
    taken = jnp.where(live[:, None], taken, jnp.zeros_like(taken))
    blocks = taken.reshape(near, per_dev, slots, taken.shape[1])
    pooled = jnp.sum(blocks, axis=2) / slot_count[:, :, None].astype(jnp.float32)
    stats = jnp.stack([jnp.sum(pooled * pooled, axis=2), jnp.max(pooled, axis=2)])
    stats = lax.all_gather(stats[None], ("far", "near", "tp"), axis=0, tiled=True)
    stats = stats.reshape(req_count // near, -1, 2, near, per_dev)
    total_sq = jnp.sum(stats[:, :, 0], axis=1).reshape(req_count, per_dev)
    peak = jnp.max(stats[:, :, 1], axis=1).reshape(req_count, per_dev)
    offset = jnp.arange(per_dev)
    sources = jnp.mod(here - offset, req_count)
    scale = jnp.sqrt(total_sq[sources, offset] / OUT + EPS)
    own = exchange(taken.astype(jnp.bfloat16), 0, 1)
    parcels = [own[:slots]]
    for o in range(1, per_dev):
        parcels.append(shifted(own[o * slots : (o + 1) * slots], ("far", "near"), o))
    return (jnp.concatenate(parcels, axis=0), scale, peak[sources, offset] / scale)


def group_of(mesh, args):
    tp, req = mesh.shape["tp"], mesh.shape["req"]
    for near in (4, 2):
        whole = req % near == 0
        heads = args[1].shape[2] // (HD * tp)
        if whole and heads % near == 0:
            return near
    return 1


def solution(mesh):
    def step(*args):
        near = group_of(mesh, args)
        if near == 1:
            return plain_solution(mesh)(*args)
        tp, req = mesh.shape["tp"], mesh.shape["req"]
        split = jax.sharding.Mesh(
            mesh.devices.reshape(req // near, near, tp), ("far", "near", "tp")
        )
        both = ("far", "near")
        return jax.shard_map(
            grouped_shards,
            mesh=split,
            in_specs=(
                P(both, None),
                P(both, None, "tp"),
                P("tp", both),
                P(both, "tp"),
                P("tp", both),
                P(),
                P(),
                P(),
                P(both, "tp"),
                P(),
                P(),
                P(both),
                P(both),
                P(),
            ),
            out_specs=(P(both, "tp"), P(both), P(both)),
            check_vma=False,
        )(*args)

    return step
```

```python
import math

import jax
import jax.numpy as jnp
from jax import lax
from jax.sharding import PartitionSpec as P

HD = 104
OUT = 4096


EPS = 1e-06


def shifted(value, axis, steps):
    count = lax.axis_size(axis)
    pairs = [(source, (source + steps) % count) for source in range(count)]
    return lax.ppermute(value, axis, pairs)


def layer_norm(rows, gain):
    mean = jnp.mean(rows, axis=-1, keepdims=True)
    centered = rows - mean
    spread = jnp.mean(centered * centered, axis=-1, keepdims=True)
    return (centered * lax.rsqrt(spread + EPS) * gain).astype(jnp.bfloat16)


def attend(qkv_rows, segment_ids, patch_mask, head_dim):
    count = qkv_rows.shape[0]
    heads = qkv_rows.shape[2] // head_dim
    split = qkv_rows.reshape(count, 3, heads, head_dim)
    query, keys, values = (split[:, 0], split[:, 1], split[:, 2])
    scores = jnp.einsum(
        "qhd,khd->hqk", query, keys, preferred_element_type=jnp.float32
    ) / math.sqrt(head_dim)
    places = jnp.arange(count)
    visible = (segment_ids[:, None] == segment_ids[None, :]) & (patch_mask[None, :] > 0) | (
        places[:, None] == places[None, :]
    )
    scores = jnp.where(visible[None], scores, -1e30)
    peak = jnp.max(scores, axis=-1, keepdims=True)
    weights = jnp.exp(scores - peak)
    total = jnp.sum(weights, axis=-1, keepdims=True)
    probs = (weights / total).astype(jnp.bfloat16)
    mixed = jnp.einsum("hqk,khd->qhd", probs, values, preferred_element_type=jnp.float32)
    return mixed.astype(jnp.bfloat16).reshape(count, heads * head_dim)


def shards(
    tokens,
    qkv_weight,
    out_weight,
    fc1_weight,
    fc2_weight,
    norm1_gain,
    norm2_gain,
    norm3_gain,
    proj_weight,
    grid_h,
    grid_w,
    segment_ids,
    patch_mask,
    owner,
):
    rows = tokens.shape[0]
    width = tokens.shape[1]
    share = rows // lax.axis_size("tp")
    resid = tokens.astype(jnp.float32)
    normed = layer_norm(resid, norm1_gain)
    columns = normed
    qkv_rows = jnp.einsum(
        "rd,dcj->rcj",
        columns,
        lax.all_gather(qkv_weight, "req", axis=0, tiled=True),
        preferred_element_type=jnp.float32,
    ).astype(jnp.bfloat16)
    mixed = attend(qkv_rows, segment_ids, patch_mask, HD)
    attn_part = jnp.dot(
        mixed,
        lax.all_gather(out_weight, "req", axis=1, tiled=True),
        preferred_element_type=jnp.float32,
    )
    first = lax.axis_index("tp") * share
    resid1 = lax.dynamic_slice_in_dim(resid, first, share, 0) + lax.psum_scatter(
        attn_part, "tp", scatter_dimension=0, tiled=True
    )
    normed2 = lax.all_gather(layer_norm(resid1, norm2_gain), "tp", axis=0, tiled=True)
    columns = normed2
    before = jnp.dot(
        columns,
        lax.all_gather(fc1_weight, "req", axis=0, tiled=True),
        preferred_element_type=jnp.float32,
    )
    hidden = jax.nn.gelu(before, approximate=False).astype(jnp.bfloat16)
    resid2 = resid1 + lax.psum_scatter(
        jnp.dot(
            hidden,
            lax.all_gather(fc2_weight, "req", axis=1, tiled=True),
            preferred_element_type=jnp.float32,
        ),
        "tp",
        scatter_dimension=0,
        tiled=True,
    )
    final = lax.all_gather(layer_norm(resid2, norm3_gain), "tp", axis=0, tiled=True)
    merged = final.reshape(rows // 4, 4 * width)
    req_count = lax.axis_size("req")
    here = lax.axis_index("req")
    per_dev = grid_h.shape[0] // req_count
    slots = rows // (4 * per_dev)
    merged_len = grid_h * grid_w // 4
    mine = lax.dynamic_slice_in_dim(merged_len, here * per_dev, per_dev)
    my_owner = lax.dynamic_slice_in_dim(owner, here * per_dev, per_dev)
    my_start = jnp.cumsum(mine) - mine
    offsets = jnp.mod(my_owner - here, req_count)
    pick = offsets[None, :] == jnp.arange(per_dev)[:, None]
    send_start = jnp.sum(jnp.where(pick, my_start[None, :], 0), axis=1)
    send_count = jnp.sum(jnp.where(pick, mine[None, :], 0), axis=1)
    step_index = jnp.arange(slots)
    source_of = jnp.arange(grid_h.shape[0]) // per_dev
    sources = jnp.mod(here - jnp.arange(per_dev), req_count)
    match = (owner[None, :] == here) & (source_of[None, :] == sources[:, None])
    recv_count = jnp.sum(jnp.where(match, merged_len[None, :], 0), axis=1)

    def slot_rows(table, offset):
        index = jnp.minimum(send_start[offset] + step_index, table.shape[0] - 1)
        taken = jnp.take(table, index, axis=0)
        return jnp.where((step_index < send_count[offset])[:, None], taken, jnp.zeros_like(taken))

    def project_rows(inputs):

        def add_proj(total, piece, start):
            return jnp.dot(inputs, piece, preferred_element_type=jnp.float32)

        return (add_proj, jnp.zeros((inputs.shape[0], proj_weight.shape[1]), jnp.float32))

    parcels = [slot_rows(merged, 0)]
    offset = 1
    parcels.append(shifted(slot_rows(merged, offset), "req", offset))
    owned = jnp.concatenate(parcels, axis=0)
    add_proj, proj_init = project_rows(owned)
    projected = add_proj(
        proj_init, lax.all_gather(proj_weight, "req", axis=0, tiled=True), jnp.int32(0)
    )
    blocks = projected.reshape(per_dev, slots, projected.shape[1])
    pooled = jnp.sum(blocks, axis=1) / recv_count[:, None].astype(jnp.float32)
    squares = jnp.sum(pooled * pooled, axis=1)
    largest = jnp.max(pooled, axis=1)
    total_sq = lax.psum(squares, "tp")
    peak = lax.pmax(largest, "tp")
    scale = jnp.sqrt(total_sq / OUT + EPS)
    return (projected.astype(jnp.bfloat16), scale, peak / scale)


def plain_solution(mesh):
    return jax.shard_map(
        shards,
        mesh=mesh,
        in_specs=(
            P("req", None),
            P("req", None, "tp"),
            P("tp", "req"),
            P("req", "tp"),
            P("tp", "req"),
            P(),
            P(),
            P(),
            P("req", "tp"),
            P(),
            P(),
            P("req"),
            P("req"),
            P(),
        ),
        out_specs=(P("req", "tp"), P("req"), P("req")),
        check_vma=False,
    )


def attend_group(qkv_rows, segment_ids, key_ids, head_dim):
    parts, count = segment_ids.shape
    heads = qkv_rows.shape[2] // head_dim
    split = qkv_rows.reshape(parts, count, 3, heads, head_dim)
    query, keys, values = (split[:, :, 0], split[:, :, 1], split[:, :, 2])
    scores = jnp.einsum(
        "gqhd,gkhd->ghqk", query, keys, preferred_element_type=jnp.float32
    ) / math.sqrt(head_dim)
    places = jnp.arange(count)
    visible = (segment_ids[:, :, None] == key_ids[:, None, :]) | (
        places[:, None] == places[None, :]
    )
    scores = jnp.where(visible[:, None], scores, -1e30)
    peak = jnp.max(scores, axis=-1, keepdims=True)
    weights = jnp.exp(scores - peak)
    total = jnp.sum(weights, axis=-1, keepdims=True)
    probs = (weights / total).astype(jnp.bfloat16)
    mixed = jnp.einsum("ghqk,gkhd->gqhd", probs, values, preferred_element_type=jnp.float32)
    return mixed.astype(jnp.bfloat16).reshape(parts * count, heads * head_dim)


def exchange(value, split_axis, concat_axis):
    return lax.all_to_all(value, "near", split_axis, concat_axis, tiled=True)


def ring_pairs(order):
    ahead = [(order[p], order[(p + 1) % 4]) for p in range(4)]
    return ahead, [(target, source) for source, target in ahead]


def ring_first(value, axis, order):
    if lax.axis_size(axis) != 4:
        return (value,)
    ahead, behind = ring_pairs(order)
    return value, lax.ppermute(value, axis, ahead), lax.ppermute(value, axis, behind)


def ring_second(blocks, axis, order):
    if lax.axis_size(axis) != 4:
        return lax.all_gather(blocks[0], axis, axis=0, tiled=False)
    value, left, right = blocks
    ahead, behind = ring_pairs(order)
    half = value.shape[0] // 2
    upper = lax.ppermute(left[:half], axis, ahead)
    lower = lax.ppermute(right[half:], axis, behind)
    me = lax.axis_index(axis)
    names = jnp.array(order)
    place = jnp.sum(jnp.where(names == me, jnp.arange(4), 0))

    def member(steps):
        return jnp.sum(jnp.where(jnp.arange(4) == jnp.mod(place + steps, 4), names, 0))

    out = jnp.zeros((4,) + value.shape, value.dtype)
    rest = (0,) * (value.ndim - 1)
    out = lax.dynamic_update_slice(out, value[None], (me, 0) + rest)
    out = lax.dynamic_update_slice(out, left[None], (member(3), 0) + rest)
    out = lax.dynamic_update_slice(out, right[None], (member(1), 0) + rest)
    out = lax.dynamic_update_slice(out, upper[None], (member(2), 0) + rest)
    return lax.dynamic_update_slice(out, lower[None], (member(2), half) + rest)


LINE = (0, 1, 2, 3)
PLANE = (0, 1, 3, 2)


def far_first(value):
    return ring_first(value, "far", LINE)


def far_second(blocks):
    out = ring_second(blocks, "far", LINE)
    return out.reshape((-1,) + out.shape[2:])


def gather_group(value):
    return lax.all_gather(value, ("near", "tp"), axis=0, tiled=True)


def grouped_shards(
    tokens,
    qkv_weight,
    out_weight,
    fc1_weight,
    fc2_weight,
    norm1_gain,
    norm2_gain,
    norm3_gain,
    proj_weight,
    grid_h,
    grid_w,
    segment_ids,
    patch_mask,
    owner,
):
    rows, width = tokens.shape
    near = lax.axis_size("near")
    req_count = lax.axis_size("far") * near
    group_first = lax.axis_index("far") * near
    share = rows // lax.axis_size("tp")
    first = lax.axis_index("tp") * share

    near_heads = qkv_weight.shape[2] // near
    qkv_cut = qkv_weight.reshape(-1, 3, near, near_heads).transpose(2, 0, 1, 3)
    qkv_cut = qkv_cut.reshape(near * qkv_weight.shape[0], 3 * near_heads)
    qkv, fc1_weight, fc2_weight, proj_weight, out_weight = lax.optimization_barrier(
        (exchange(qkv_cut, 0, 0), fc1_weight, fc2_weight, proj_weight, out_weight)
    )
    qkv_full = far_second(far_first(qkv))
    fc1 = exchange(fc1_weight, 1, 0)
    fc2 = exchange(fc2_weight.T, 1, 0)
    proj = exchange(proj_weight, 1, 0)

    ids = jnp.stack([segment_ids, jnp.where(patch_mask > 0, segment_ids, -1)])[None]
    ids = exchange(jnp.broadcast_to(ids, (near,) + ids.shape[1:]), 0, 0)
    resid = lax.dynamic_slice_in_dim(tokens, first, share, 0).astype(jnp.float32)
    normed = gather_group(layer_norm(resid, norm1_gain))
    normed, fc1, fc2 = lax.optimization_barrier((normed, fc1, fc2))
    fc1, fc2 = far_first(fc1), far_first(fc2)
    out_far = ring_second(ring_first(out_weight.T, "far", LINE), "far", LINE)
    out_near = ring_first(out_far, "near", PLANE)
    qkv_rows = jnp.dot(normed, qkv_full, preferred_element_type=jnp.float32).astype(jnp.bfloat16)
    qkv_rows = qkv_rows.reshape(-1, 3, near_heads)
    mixed = attend_group(qkv_rows, ids[:, 0], ids[:, 1], HD)
    mixed, proj, out_near, fc1 = lax.optimization_barrier((mixed, proj, out_near, fc1))
    fc1_full = far_second(fc1)
    mixed = exchange(mixed, 0, 1)
    out_full = jnp.swapaxes(ring_second(out_near, "near", PLANE), 0, 1)
    out_full = out_full.reshape(width, out_weight.shape[0])
    attn_part = jnp.einsum("rk,ck->rc", mixed, out_full, preferred_element_type=jnp.float32)
    resid1 = resid + lax.psum_scatter(attn_part, "tp", scatter_dimension=0, tiled=True)
    resid1, fc1_full, fc2 = lax.optimization_barrier((resid1, fc1_full, fc2))
    fc2_full = far_second(fc2)
    normed2 = gather_group(layer_norm(resid1, norm2_gain))
    normed2, proj = lax.optimization_barrier((normed2, proj))
    proj = far_first(proj)
    before = jnp.dot(normed2, fc1_full, preferred_element_type=jnp.float32)
    hidden = jax.nn.gelu(before, approximate=False).astype(jnp.bfloat16)
    resid2 = resid1 + lax.psum_scatter(
        jnp.einsum("rk,ck->rc", hidden, fc2_full, preferred_element_type=jnp.float32),
        ("near", "tp"),
        scatter_dimension=0,
        tiled=True,
    )
    resid2, proj = lax.optimization_barrier((resid2, proj))
    proj_full = far_second(proj)
    merged = gather_group(layer_norm(resid2, norm3_gain).reshape(share // 4, 4 * width))
    projected = jnp.dot(merged, proj_full, preferred_element_type=jnp.float32)

    per_dev = grid_h.shape[0] // req_count
    places = rows // 4
    slots = places // per_dev
    merged_len = (grid_h * grid_w // 4).reshape(req_count, per_dev)
    starts = jnp.cumsum(merged_len, axis=1) - merged_len
    offsets = jnp.mod(owner.reshape(req_count, per_dev) - jnp.arange(req_count)[:, None], req_count)
    pick = offsets[:, None, :] == jnp.arange(per_dev)[None, :, None]
    slot_start = jnp.sum(jnp.where(pick, starts[:, None, :], 0), axis=2)
    slot_count = jnp.sum(jnp.where(pick, merged_len[:, None, :], 0), axis=2)
    slot_start = lax.dynamic_slice_in_dim(slot_start, group_first, near, 0)
    slot_count = lax.dynamic_slice_in_dim(slot_count, group_first, near, 0)
    step = jnp.arange(slots)
    index = jnp.minimum(slot_start[:, :, None] + step, places - 1)
    index = index + (jnp.arange(near) * places)[:, None, None]
    taken = jnp.take(projected, index.reshape(-1), axis=0)
    live = (step < slot_count[:, :, None]).reshape(-1)
    taken = jnp.where(live[:, None], taken, jnp.zeros_like(taken))
    blocks = taken.reshape(near, per_dev, slots, taken.shape[1])
    pooled = jnp.sum(blocks, axis=2) / slot_count[:, :, None].astype(jnp.float32)
    pooled = exchange(pooled, 0, 2)[0]
    stats = jnp.stack([jnp.sum(pooled * pooled, axis=1), jnp.max(pooled, axis=1)])
    own = exchange(taken.astype(jnp.bfloat16), 0, 1)
    parcels = [own[:slots]]
    marks = [stats[:, :1]]
    for o in range(1, per_dev):
        parcels.append(shifted(own[o * slots : (o + 1) * slots], ("far", "near"), o))
        marks.append(shifted(stats[:, o : o + 1], ("far", "near"), o))
    marks = jnp.concatenate(marks, axis=1)
    scale = jnp.sqrt(lax.psum(marks[0], "tp") / OUT + EPS)
    return (jnp.concatenate(parcels, axis=0), scale, lax.pmax(marks[1], "tp") / scale)


def group_of(mesh, args):
    tp, req = mesh.shape["tp"], mesh.shape["req"]
    for near in (4, 2):
        whole = req % near == 0
        heads = args[1].shape[2] // (HD * tp)
        if whole and heads % near == 0:
            return near
    return 1


def solution(mesh):
    def step(*args):
        near = group_of(mesh, args)
        if near == 1:
            return plain_solution(mesh)(*args)
        tp, req = mesh.shape["tp"], mesh.shape["req"]
        split = jax.sharding.Mesh(
            mesh.devices.reshape(req // near, near, tp), ("far", "near", "tp")
        )
        both = ("far", "near")
        return jax.shard_map(
            grouped_shards,
            mesh=split,
            in_specs=(
                P(both, None),
                P(both, None, "tp"),
                P("tp", both),
                P(both, "tp"),
                P("tp", both),
                P(),
                P(),
                P(),
                P(both, "tp"),
                P(),
                P(),
                P(both),
                P(both),
                P(),
            ),
            out_specs=(P(both, "tp"), P(both), P(both)),
            check_vma=False,
        )(*args)

    return step
```

```python
import math

import jax
import jax.numpy as jnp
from jax import lax
from jax.sharding import PartitionSpec as P

HD = 104
OUT = 4096


EPS = 1e-06


def shifted(value, axis, steps):
    count = lax.axis_size(axis)
    pairs = [(source, (source + steps) % count) for source in range(count)]
    return lax.ppermute(value, axis, pairs)


def layer_norm(rows, gain):
    mean = jnp.mean(rows, axis=-1, keepdims=True)
    centered = rows - mean
    spread = jnp.mean(centered * centered, axis=-1, keepdims=True)
    return (centered * lax.rsqrt(spread + EPS) * gain).astype(jnp.bfloat16)


def attend(qkv_rows, segment_ids, patch_mask, head_dim):
    count = qkv_rows.shape[0]
    heads = qkv_rows.shape[2] // head_dim
    split = qkv_rows.reshape(count, 3, heads, head_dim)
    query, keys, values = (split[:, 0], split[:, 1], split[:, 2])
    scores = jnp.einsum(
        "qhd,khd->hqk", query, keys, preferred_element_type=jnp.float32
    ) / math.sqrt(head_dim)
    places = jnp.arange(count)
    visible = (segment_ids[:, None] == segment_ids[None, :]) & (patch_mask[None, :] > 0) | (
        places[:, None] == places[None, :]
    )
    scores = jnp.where(visible[None], scores, -1e30)
    peak = jnp.max(scores, axis=-1, keepdims=True)
    weights = jnp.exp(scores - peak)
    total = jnp.sum(weights, axis=-1, keepdims=True)
    probs = (weights / total).astype(jnp.bfloat16)
    mixed = jnp.einsum("hqk,khd->qhd", probs, values, preferred_element_type=jnp.float32)
    return mixed.astype(jnp.bfloat16).reshape(count, heads * head_dim)


def shards(
    tokens,
    qkv_weight,
    out_weight,
    fc1_weight,
    fc2_weight,
    norm1_gain,
    norm2_gain,
    norm3_gain,
    proj_weight,
    grid_h,
    grid_w,
    segment_ids,
    patch_mask,
    owner,
):
    rows = tokens.shape[0]
    width = tokens.shape[1]
    share = rows // lax.axis_size("tp")
    resid = tokens.astype(jnp.float32)
    normed = layer_norm(resid, norm1_gain)
    columns = normed
    qkv_rows = jnp.einsum(
        "rd,dcj->rcj",
        columns,
        lax.all_gather(qkv_weight, "req", axis=0, tiled=True),
        preferred_element_type=jnp.float32,
    ).astype(jnp.bfloat16)
    mixed = attend(qkv_rows, segment_ids, patch_mask, HD)
    attn_part = jnp.dot(
        mixed,
        lax.all_gather(out_weight, "req", axis=1, tiled=True),
        preferred_element_type=jnp.float32,
    )
    first = lax.axis_index("tp") * share
    resid1 = lax.dynamic_slice_in_dim(resid, first, share, 0) + lax.psum_scatter(
        attn_part, "tp", scatter_dimension=0, tiled=True
    )
    normed2 = lax.all_gather(layer_norm(resid1, norm2_gain), "tp", axis=0, tiled=True)
    columns = normed2
    before = jnp.dot(
        columns,
        lax.all_gather(fc1_weight, "req", axis=0, tiled=True),
        preferred_element_type=jnp.float32,
    )
    hidden = jax.nn.gelu(before, approximate=False).astype(jnp.bfloat16)
    resid2 = resid1 + lax.psum_scatter(
        jnp.dot(
            hidden,
            lax.all_gather(fc2_weight, "req", axis=1, tiled=True),
            preferred_element_type=jnp.float32,
        ),
        "tp",
        scatter_dimension=0,
        tiled=True,
    )
    final = lax.all_gather(layer_norm(resid2, norm3_gain), "tp", axis=0, tiled=True)
    merged = final.reshape(rows // 4, 4 * width)
    req_count = lax.axis_size("req")
    here = lax.axis_index("req")
    per_dev = grid_h.shape[0] // req_count
    slots = rows // (4 * per_dev)
    merged_len = grid_h * grid_w // 4
    mine = lax.dynamic_slice_in_dim(merged_len, here * per_dev, per_dev)
    my_owner = lax.dynamic_slice_in_dim(owner, here * per_dev, per_dev)
    my_start = jnp.cumsum(mine) - mine
    offsets = jnp.mod(my_owner - here, req_count)
    pick = offsets[None, :] == jnp.arange(per_dev)[:, None]
    send_start = jnp.sum(jnp.where(pick, my_start[None, :], 0), axis=1)
    send_count = jnp.sum(jnp.where(pick, mine[None, :], 0), axis=1)
    step_index = jnp.arange(slots)
    source_of = jnp.arange(grid_h.shape[0]) // per_dev
    sources = jnp.mod(here - jnp.arange(per_dev), req_count)
    match = (owner[None, :] == here) & (source_of[None, :] == sources[:, None])
    recv_count = jnp.sum(jnp.where(match, merged_len[None, :], 0), axis=1)

    def slot_rows(table, offset):
        index = jnp.minimum(send_start[offset] + step_index, table.shape[0] - 1)
        taken = jnp.take(table, index, axis=0)
        return jnp.where((step_index < send_count[offset])[:, None], taken, jnp.zeros_like(taken))

    def project_rows(inputs):

        def add_proj(total, piece, start):
            return jnp.dot(inputs, piece, preferred_element_type=jnp.float32)

        return (add_proj, jnp.zeros((inputs.shape[0], proj_weight.shape[1]), jnp.float32))

    parcels = [slot_rows(merged, 0)]
    offset = 1
    parcels.append(shifted(slot_rows(merged, offset), "req", offset))
    owned = jnp.concatenate(parcels, axis=0)
    add_proj, proj_init = project_rows(owned)
    projected = add_proj(
        proj_init, lax.all_gather(proj_weight, "req", axis=0, tiled=True), jnp.int32(0)
    )
    blocks = projected.reshape(per_dev, slots, projected.shape[1])
    pooled = jnp.sum(blocks, axis=1) / recv_count[:, None].astype(jnp.float32)
    squares = jnp.sum(pooled * pooled, axis=1)
    largest = jnp.max(pooled, axis=1)
    total_sq = lax.psum(squares, "tp")
    peak = lax.pmax(largest, "tp")
    scale = jnp.sqrt(total_sq / OUT + EPS)
    return (projected.astype(jnp.bfloat16), scale, peak / scale)


def plain_solution(mesh):
    return jax.shard_map(
        shards,
        mesh=mesh,
        in_specs=(
            P("req", None),
            P("req", None, "tp"),
            P("tp", "req"),
            P("req", "tp"),
            P("tp", "req"),
            P(),
            P(),
            P(),
            P("req", "tp"),
            P(),
            P(),
            P("req"),
            P("req"),
            P(),
        ),
        out_specs=(P("req", "tp"), P("req"), P("req")),
        check_vma=False,
    )


def attend_group(qkv_rows, segment_ids, key_ids, head_dim):
    parts, count = segment_ids.shape
    heads = qkv_rows.shape[2] // head_dim
    split = qkv_rows.reshape(parts, count, 3, heads, head_dim)
    query, keys, values = (split[:, :, 0], split[:, :, 1], split[:, :, 2])
    scores = jnp.einsum(
        "gqhd,gkhd->ghqk", query, keys, preferred_element_type=jnp.float32
    ) / math.sqrt(head_dim)
    places = jnp.arange(count)
    visible = (segment_ids[:, :, None] == key_ids[:, None, :]) | (
        places[:, None] == places[None, :]
    )
    scores = jnp.where(visible[:, None], scores, -1e30)
    peak = jnp.max(scores, axis=-1, keepdims=True)
    weights = jnp.exp(scores - peak)
    total = jnp.sum(weights, axis=-1, keepdims=True)
    probs = (weights / total).astype(jnp.bfloat16)
    mixed = jnp.einsum("ghqk,gkhd->gqhd", probs, values, preferred_element_type=jnp.float32)
    return mixed.astype(jnp.bfloat16).reshape(parts * count, heads * head_dim)


def exchange(value, split_axis, concat_axis):
    return lax.all_to_all(value, "near", split_axis, concat_axis, tiled=True)


def ring_pairs(order):
    ahead = [(order[p], order[(p + 1) % 4]) for p in range(4)]
    return ahead, [(target, source) for source, target in ahead]


def ring_first(value, axis, order):
    if lax.axis_size(axis) != 4:
        return (value,)
    ahead, behind = ring_pairs(order)
    return value, lax.ppermute(value, axis, ahead), lax.ppermute(value, axis, behind)


def ring_second(blocks, axis, order):
    if lax.axis_size(axis) != 4:
        return lax.all_gather(blocks[0], axis, axis=0, tiled=False)
    value, left, right = blocks
    ahead, behind = ring_pairs(order)
    half = value.shape[0] // 2
    upper = lax.ppermute(left[:half], axis, ahead)
    lower = lax.ppermute(right[half:], axis, behind)
    me = lax.axis_index(axis)
    names = jnp.array(order)
    place = jnp.sum(jnp.where(names == me, jnp.arange(4), 0))

    def member(steps):
        return jnp.sum(jnp.where(jnp.arange(4) == jnp.mod(place + steps, 4), names, 0))

    out = jnp.zeros((4,) + value.shape, value.dtype)
    rest = (0,) * (value.ndim - 1)
    out = lax.dynamic_update_slice(out, value[None], (me, 0) + rest)
    out = lax.dynamic_update_slice(out, left[None], (member(3), 0) + rest)
    out = lax.dynamic_update_slice(out, right[None], (member(1), 0) + rest)
    out = lax.dynamic_update_slice(out, upper[None], (member(2), 0) + rest)
    return lax.dynamic_update_slice(out, lower[None], (member(2), half) + rest)


LINE = (0, 1, 2, 3)
PLANE = (0, 1, 3, 2)


def far_first(value):
    return ring_first(value, "far", LINE)


def far_second(blocks):
    out = ring_second(blocks, "far", LINE)
    return out.reshape((-1,) + out.shape[2:])


def gather_group(value):
    return lax.all_gather(value, ("near", "tp"), axis=0, tiled=True)


def grouped_shards(
    tokens,
    qkv_weight,
    out_weight,
    fc1_weight,
    fc2_weight,
    norm1_gain,
    norm2_gain,
    norm3_gain,
    proj_weight,
    grid_h,
    grid_w,
    segment_ids,
    patch_mask,
    owner,
):
    rows, width = tokens.shape
    near = lax.axis_size("near")
    req_count = lax.axis_size("far") * near
    group_first = lax.axis_index("far") * near
    share = rows // lax.axis_size("tp")
    first = lax.axis_index("tp") * share

    near_heads = qkv_weight.shape[2] // near
    qkv_cut = qkv_weight.reshape(-1, 3, near, near_heads).transpose(2, 0, 1, 3)
    qkv_cut = qkv_cut.reshape(near * qkv_weight.shape[0], 3 * near_heads)
    qkv, fc1_weight, fc2_weight, proj_weight, out_weight = lax.optimization_barrier(
        (exchange(qkv_cut, 0, 0), fc1_weight, fc2_weight, proj_weight, out_weight)
    )
    qkv_full = far_second(far_first(qkv))
    fc1 = exchange(fc1_weight, 1, 0)
    fc2 = exchange(fc2_weight.T, 1, 0)
    proj = exchange(proj_weight, 1, 0)

    ids = jnp.stack([segment_ids, jnp.where(patch_mask > 0, segment_ids, -1)])[None]
    ids = exchange(jnp.broadcast_to(ids, (near,) + ids.shape[1:]), 0, 0)
    resid = lax.dynamic_slice_in_dim(tokens, first, share, 0).astype(jnp.float32)
    normed = gather_group(layer_norm(resid, norm1_gain))
    normed, fc1, fc2, out_weight = lax.optimization_barrier((normed, fc1, fc2, out_weight))
    fc1 = far_first(fc1)
    out_far = ring_second(ring_first(out_weight.T, "far", LINE), "far", LINE)
    out_near = ring_first(out_far, "near", PLANE)
    qkv_rows = jnp.dot(normed, qkv_full, preferred_element_type=jnp.float32).astype(jnp.bfloat16)
    qkv_rows = qkv_rows.reshape(-1, 3, near_heads)
    mixed = attend_group(qkv_rows, ids[:, 0], ids[:, 1], HD)
    mixed, proj, out_near, fc1 = lax.optimization_barrier((mixed, proj, out_near, fc1))
    fc1_full = far_second(fc1)
    mixed = exchange(mixed, 0, 1)
    out_full = jnp.swapaxes(ring_second(out_near, "near", PLANE), 0, 1)
    out_full = out_full.reshape(width, out_weight.shape[0])
    attn_part = jnp.einsum("rk,ck->rc", mixed, out_full, preferred_element_type=jnp.float32)
    resid1 = resid + lax.psum_scatter(attn_part, "tp", scatter_dimension=0, tiled=True)
    resid1, fc1_full, fc2 = lax.optimization_barrier((resid1, fc1_full, fc2))
    fc2 = far_first(fc2)
    normed2 = gather_group(layer_norm(resid1, norm2_gain))
    normed2, proj, fc2 = lax.optimization_barrier((normed2, proj, fc2))
    fc2_full = far_second(fc2)
    proj = far_first(proj)
    before = jnp.dot(normed2, fc1_full, preferred_element_type=jnp.float32)
    hidden = jax.nn.gelu(before, approximate=False).astype(jnp.bfloat16)
    hidden, fc2_full = lax.optimization_barrier((hidden, fc2_full))
    resid2 = resid1 + lax.psum_scatter(
        jnp.einsum("rk,ck->rc", hidden, fc2_full, preferred_element_type=jnp.float32),
        ("near", "tp"),
        scatter_dimension=0,
        tiled=True,
    )
    resid2, proj = lax.optimization_barrier((resid2, proj))
    proj_full = far_second(proj)
    merged = gather_group(layer_norm(resid2, norm3_gain).reshape(share // 4, 4 * width))
    projected = jnp.dot(merged, proj_full, preferred_element_type=jnp.float32)

    per_dev = grid_h.shape[0] // req_count
    places = rows // 4
    slots = places // per_dev
    merged_len = (grid_h * grid_w // 4).reshape(req_count, per_dev)
    starts = jnp.cumsum(merged_len, axis=1) - merged_len
    offsets = jnp.mod(owner.reshape(req_count, per_dev) - jnp.arange(req_count)[:, None], req_count)
    pick = offsets[:, None, :] == jnp.arange(per_dev)[None, :, None]
    slot_start = jnp.sum(jnp.where(pick, starts[:, None, :], 0), axis=2)
    slot_count = jnp.sum(jnp.where(pick, merged_len[:, None, :], 0), axis=2)
    slot_start = lax.dynamic_slice_in_dim(slot_start, group_first, near, 0)
    slot_count = lax.dynamic_slice_in_dim(slot_count, group_first, near, 0)
    step = jnp.arange(slots)
    index = jnp.minimum(slot_start[:, :, None] + step, places - 1)
    index = index + (jnp.arange(near) * places)[:, None, None]
    taken = jnp.take(projected, index.reshape(-1), axis=0)
    live = (step < slot_count[:, :, None]).reshape(-1)
    taken = jnp.where(live[:, None], taken, jnp.zeros_like(taken))
    blocks = taken.reshape(near, per_dev, slots, taken.shape[1])
    pooled = jnp.sum(blocks, axis=2) / slot_count[:, :, None].astype(jnp.float32)
    pooled = exchange(pooled, 0, 2)[0]
    stats = jnp.stack([jnp.sum(pooled * pooled, axis=1), jnp.max(pooled, axis=1)])
    own = exchange(taken.astype(jnp.bfloat16), 0, 1)
    parcels = [own[:slots]]
    marks = [stats[:, :1]]
    for o in range(1, per_dev):
        parcels.append(shifted(own[o * slots : (o + 1) * slots], ("far", "near"), o))
        marks.append(shifted(stats[:, o : o + 1], ("far", "near"), o))
    marks = jnp.concatenate(marks, axis=1)
    scale = jnp.sqrt(lax.psum(marks[0], "tp") / OUT + EPS)
    return (jnp.concatenate(parcels, axis=0), scale, lax.pmax(marks[1], "tp") / scale)


def group_of(mesh, args):
    tp, req = mesh.shape["tp"], mesh.shape["req"]
    for near in (4, 2):
        whole = req % near == 0
        heads = args[1].shape[2] // (HD * tp)
        if whole and heads % near == 0:
            return near
    return 1


def solution(mesh):
    def step(*args):
        near = group_of(mesh, args)
        if near == 1:
            return plain_solution(mesh)(*args)
        tp, req = mesh.shape["tp"], mesh.shape["req"]
        split = jax.sharding.Mesh(
            mesh.devices.reshape(req // near, near, tp), ("far", "near", "tp")
        )
        both = ("far", "near")
        return jax.shard_map(
            grouped_shards,
            mesh=split,
            in_specs=(
                P(both, None),
                P(both, None, "tp"),
                P("tp", both),
                P(both, "tp"),
                P("tp", both),
                P(),
                P(),
                P(),
                P(both, "tp"),
                P(),
                P(),
                P(both),
                P(both),
                P(),
            ),
            out_specs=(P(both, "tp"), P(both), P(both)),
            check_vma=False,
        )(*args)

    return step
```
